32 devices in a mesh: mol: 2 (over y), band: 8 (over z, x), grid: 2 (over core).
Axes of the slice: x: 2, y: 2, z: 4, core: 2. Of those that a mesh axis runs over, the one named last changes fastest.
Arguments:
- orbitals: bfloat16 [32, 373248], P(('mol', 'band'), 'grid'), parts along dimension 0, may hold values from -6 to 6
- group_order: int32 [32], P('mol'), parts along dimension 0, may hold values from 0 to 15, each once
- localizer: bfloat16 [2, 16, 16], P('mol'), parts along dimension 0, may hold values from -1.5 to 1.5
- bond_keep: int32 [32, 1], P('mol'), parts along dimension 0, may hold values 0 or 1
Outputs:
- localized: bfloat16 [32, 373248], P(('mol', 'band', 'grid')), parts along dimension 0
- exchange_term: bfloat16 [32, 373248], P(('mol', 'band', 'grid')), parts along dimension 0
The draws below stay inside these ranges and needn't reach their ends.
There are 2 independent parts, one for each index of `mol`. The reference program is written for one: setup_inputs(seed, part) draws one part's arguments, and reference() takes and returns one part's arrays. A program takes and returns all parts, laid end to end along the dimension named above; each array names one. Nothing has to cross between parts.
Inputs may be any that keep to these rules, and one draw needn't show every extreme that they name: A permutation; localization group g holds the orbitals group_order[g * 16 + a] for a below 16. `bond_keep`: 1 keeps a pair of orbitals, 0 screens it out.
All inputs are finite; a program needn't handle non-finite values.
Results may differ from the reference program's by a relative error of at most 0.0099.
Values may be sent and summed in bfloat16 or wider, within the bound.
No kernel may reach another device: no remote copies, remote signals or barrier semaphores. Data moves between devices by JAX's collectives and lax.ppermute only.
A program may use at most 64 MiB of HBM per device.

```python
import math
import jax
import jax.numpy as jnp
from jax import lax

NG = 72
RADIUS = 1
ORBITALS = 16
GROUP = 16
NGROUPS = 1


def plant(drawn, key, low, largest):
    longest = drawn.shape.index(max(drawn.shape))
    spots = []
    for shift in (0, 1):
        where = [jax.random.randint(jax.random.fold_in(key, axis), (), 0, length) for axis, length in enumerate(drawn.shape)]
        where[longest] = (where[longest] + shift) % drawn.shape[longest]
        spots.append(tuple(where))
    return drawn.at[spots[0]].set(low).at[spots[1]].set(largest)


def steps_of(rng, dims, pieces, least, high):
    def one(position, parts):
        draws = jax.random.uniform(jax.random.fold_in(jax.random.fold_in(rng, 6), position), (parts,), jnp.float32, least / len(pieces), high / len(pieces))
        return jnp.repeat(jnp.exp(draws), dims[position] // parts).reshape((-1,) + (1,) * (len(dims) - position - 1))

    loudness = one(*pieces[0])
    for cut in pieces[1:]:
        loudness = loudness * one(*cut)
    return loudness


def normal_values(own_key, extent, spread, reach, shards=(), kind=jnp.bfloat16):
    values = jax.random.normal(own_key, extent, jnp.float32) * spread
    if len(shards) > 0:
        values = steps_of(own_key, extent, shards, -0.22, 0.18) * values
    return jnp.clip(values, min=-reach, max=reach).astype(kind)


def setup_inputs(seed: int = 0, part: int = 0) -> dict:
    key_list = jax.random.split(jax.random.key(seed), 5)
    part_splits = jax.random.split(jax.random.fold_in(key_list[4], part), 5)
    orbitals = normal_values(part_splits[0], (ORBITALS, NG * NG * NG), 1.0, 6.0, ((0, 8), (1, 2)))
    group_order = jax.random.permutation(part_splits[1], ORBITALS).astype(jnp.int32)
    localizer = normal_values(part_splits[2], (NGROUPS, GROUP, GROUP), GROUP ** -0.5, 1.5)
    bond_keep = plant((jax.random.randint(part_splits[3], (ORBITALS, RADIUS), 0, 4) < 3).astype(jnp.int32), jax.random.fold_in(part_splits[3], 1), 0, 1)
    return dict(orbitals=orbitals, group_order=group_order, localizer=localizer, bond_keep=bond_keep)


screening = 0.0625


def round_half(values):
    return lax.optimization_barrier(values.astype(jnp.bfloat16)).astype(jnp.float32)


def phase_angles(row_count, column_total):
    first_index = jnp.arange(row_count, dtype=jnp.int32)[:, None]
    second_index = jnp.arange(column_total, dtype=jnp.int32)[None, :]
    return (2.0 * math.pi / NG) * ((first_index * second_index) % NG).astype(jnp.float32)


def build_tables():
    half_count = NG // 2 + 1
    along_x = phase_angles(half_count, NG)
    x_table = jnp.stack([jnp.cos(along_x), -jnp.sin(along_x)])
    square = phase_angles(NG, NG)
    cosine_table = jnp.cos(square)
    sine_table = jnp.sin(square)
    forward_depth_axis = jnp.concatenate([jnp.concatenate([cosine_table, -sine_table], axis=1), jnp.concatenate([sine_table, cosine_table], axis=1)], axis=0)
    inverse_z = jnp.concatenate([jnp.concatenate([cosine_table, sine_table], axis=1), jnp.concatenate([-sine_table, cosine_table], axis=1)], axis=0)
    y_table = jnp.concatenate([cosine_table, sine_table], axis=0)
    half_angle = (math.pi / NG) * jnp.arange(NG, dtype=jnp.int32).astype(jnp.float32)
    symbol = 4.0 * jnp.sin(half_angle) ** 2
    denominator = screening + symbol[:half_count, None, None] + symbol[None, :, None] + symbol[None, None, :]
    x_index = jnp.arange(half_count, dtype=jnp.int32)
    weight = jnp.where((x_index == 0) | (x_index == NG // 2), 1.0, 2.0).astype(jnp.float32) / float(NG * NG * NG)
    kernel = weight[:, None, None] / denominator
    anchor = jnp.zeros((half_count, NG, NG), jnp.float32).at[0, 0, 0].set(1.0)
    kernel = kernel * (1.0 - anchor)
    kernel = jnp.concatenate([kernel, kernel], axis=2)
    return (round_half(x_table), round_half(forward_depth_axis), round_half(inverse_z), round_half(y_table), kernel)


def mix_along_y(spectrum, y_table, phase_sign):
    products = jnp.einsum("jy,kyc->kjc", y_table, spectrum, precision=lax.Precision.HIGHEST)
    cos_part = products[:, :NG]
    sin_part = products[:, NG:]
    real_part = cos_part[:, :, :NG] - phase_sign * sin_part[:, :, NG:]
    imag_part = cos_part[:, :, NG:] + phase_sign * sin_part[:, :, :NG]
    return jnp.concatenate([real_part, imag_part], axis=2)


def potential(left_field, right_field, tables):
    x_table, forward_depth_axis, inverse_z, y_table, kernel = tables
    half_count = x_table.shape[1]
    density = round_half(left_field * right_field)
    section_field = jnp.einsum("pkx,xyz->kypz", x_table, density, precision=lax.Precision.HIGHEST)
    section_field = round_half(section_field.reshape(half_count, NG, 2 * NG))
    section_field = jnp.dot(section_field.reshape(half_count * NG, 2 * NG), forward_depth_axis, precision=lax.Precision.HIGHEST, preferred_element_type=jnp.float32)
    section_field = round_half(section_field.reshape(half_count, NG, 2 * NG))
    section_field = round_half(mix_along_y(section_field, y_table, -1.0) * kernel)
    section_field = round_half(mix_along_y(section_field, y_table, 1.0))
    section_field = jnp.dot(section_field.reshape(half_count * NG, 2 * NG), inverse_z, precision=lax.Precision.HIGHEST, preferred_element_type=jnp.float32)
    section_field = round_half(section_field.reshape(half_count, NG, 2, NG))
    return jnp.einsum("pkx,kypz->xyz", x_table, section_field, precision=lax.Precision.HIGHEST)


def reference(orbitals, group_order, localizer, bond_keep):
    orbit_count = orbitals.shape[0]
    group_count = localizer.shape[0]
    group_width = localizer.shape[1]
    grouped_orbitals = orbitals[group_order].astype(jnp.float32).reshape(group_count, group_width, -1)
    rotated_field = jnp.einsum("iek,ikv->iev", localizer.astype(jnp.float32), grouped_orbitals, precision=lax.Precision.HIGHEST)
    rotated_field = rotated_field.reshape(orbit_count, -1).astype(jnp.bfloat16)
    localized = jnp.zeros_like(rotated_field).at[group_order].set(rotated_field)
    tables = build_tables()
    orbit_floats = localized.astype(jnp.float32)

    def exchange_row(orbital_index):
        own_float = orbit_floats[orbital_index].reshape(NG, NG, NG)
        exchange_sum = potential(own_float, own_float, tables) * own_float
        for offset in range(1, RADIUS + 1):
            lower_index = (orbital_index - offset) % orbit_count
            upper_partner_index = (orbital_index + offset) % orbit_count
            lower_float = orbit_floats[lower_index].reshape(NG, NG, NG)
            upper_partner_float = orbit_floats[upper_partner_index].reshape(NG, NG, NG)
            lower_flag = bond_keep[orbital_index, offset - 1].astype(jnp.float32)
            upper_flag = bond_keep[upper_partner_index, offset - 1].astype(jnp.float32)
            exchange_sum = exchange_sum + lower_flag * potential(own_float, lower_float, tables) * lower_float
            exchange_sum = exchange_sum + upper_flag * potential(own_float, upper_partner_float, tables) * upper_partner_float
        return exchange_sum.reshape(-1).astype(jnp.bfloat16)

    exchange_term = lax.map(exchange_row, jnp.arange(orbit_count, dtype=jnp.int32))
    return (localized, exchange_term)
```

```python
import math, functools
import numpy as np
import jax, jax.numpy as jnp
from jax import lax
from jax.experimental import pallas as pl
from jax.experimental.pallas import tpu as pltpu
from jax.sharding import PartitionSpec as P

NG = 72
HC = NG // 2 + 1
LANES = 128
KPAD = 40
XPAIRS = NG // 2
PAIR_ROWS = 2 * NG * NG // LANES
FLAT_ROWS = NG * NG * NG // LANES
FLAT_ALLOC = PAIR_ROWS * (KPAD + 1) + 7
SCREEN = 0.0625

def tables_np():
    ang = lambda r, c: 2.0 * math.pi / NG * ((np.arange(r)[:, None] * np.arange(c)[None, :]) % NG)
    ax = ang(HC, NG)
    xt = np.stack([np.cos(ax), -np.sin(ax)])
    xf = np.zeros((2, KPAD, 2, KPAD))
    xf[:, :HC, :, :XPAIRS] = xt.reshape(2, HC, XPAIRS, 2).transpose(0, 1, 3, 2)
    xf = xf.reshape(2 * KPAD, 2 * KPAD)
    c, s = np.cos(ang(NG, NG)), np.sin(ang(NG, NG))
    def pad(b):
        out = np.zeros((2, LANES, 2, LANES))
        for i in range(2):
            for j in range(2):
                out[i, :NG, j, :NG] = b[i][j]
        return out.reshape(2 * LANES, 2 * LANES)
    fz = pad([[c, -s], [s, c]])
    iz = pad([[c, s], [-s, c]])
    yf = np.block([[c, s], [-s, c]])
    yi = np.block([[c, -s], [s, c]])
    sym = 4.0 * np.sin(math.pi / NG * np.arange(NG)) ** 2
    w = np.where((np.arange(HC) == 0) | (np.arange(HC) == NG // 2), 1.0, 2.0) / float(NG ** 3)
    kern = w[:, None, None] / (SCREEN + sym[:HC, None, None] + sym[None, :, None] + sym[None, None, :])
    kern[0, 0, 0] = 0.0
    kp = np.zeros((KPAD, NG, LANES))
    kp[:HC, :, :NG] = kern
    kp = kp.reshape(KPAD // 2, 2, NG, LANES).transpose(0, 2, 1, 3).reshape(KPAD // 2 * NG, 2 * LANES)
    b = lambda a: a.astype(np.float32).astype(jnp.bfloat16)
    return b(xf), b(xf.T), b(fz), b(iz), b(yf), b(yi), kp.astype(np.float32)

def dot(a, b):
    return jnp.dot(a, b, preferred_element_type=jnp.float32)

def cat(parts, axis):
    return jnp.concatenate(parts, axis=axis)

def potential_in_flat(flat, zre, zim, s3, x2, tabs, ZCH=10):
    xf, xi, fz, iz, yf, yi, kern = tabs
    lane = lax.broadcasted_iota(jnp.int32, (KPAD, LANES), 1)

    def piece(x0, y):
        t, s = divmod(NG * (NG * x0 + y), LANES)
        a = flat[pl.ds(t, KPAD, stride=PAIR_ROWS), :]
        if s + NG > LANES:
            b = flat[pl.ds(t + 1, KPAD, stride=PAIR_ROWS), :]
            a = jnp.where(lane >= s, a, b)
        if s:
            a = pltpu.roll(a, LANES - s, 1)
        return a

    xfv = xf[...]
    for yp in range(NG // 2):
        cols = [cat([piece(0, 2 * yp + q), piece(1, 2 * yp + q)], 0) for q in range(2)]
        res = dot(xfv, cat(cols, 1).astype(jnp.bfloat16))
        for q in range(2):
            for p, z in enumerate((zre, zim)):
                z[pl.ds(2 * yp + q, KPAD, stride=NG), :] = res[p * KPAD:(p + 1) * KPAD, q * LANES:(q + 1) * LANES]

    fzv = fz[...]
    for ch in range(KPAD // ZCH):
        rows = pl.ds(ch * ZCH * NG, ZCH * NG)
        res = dot(cat([zre[rows, :], zim[rows, :]], 1).astype(jnp.bfloat16), fzv)
        for kk in range(ZCH):
            kp, kpar = divmod(ch * ZCH + kk, 2)
            for p in range(2):
                s3[pl.ds(kp * 2 * NG + p * NG, NG), kpar * LANES:(kpar + 1) * LANES] = res[kk * NG:(kk + 1) * NG, p * LANES:(p + 1) * LANES]

    yfv, yiv = yf[...], yi[...]
    for kp in range(KPAD // 2):
        w = s3[pl.ds(kp * 2 * NG, 2 * NG), :].astype(jnp.bfloat16)
        t = dot(yfv, w)
        kk = kern[pl.ds(kp * NG, NG), :]
        t = cat([t[:NG] * kk, t[NG:] * kk], 0).astype(jnp.bfloat16)
        v = dot(yiv, t)
        for kpar in range(2):
            for p, z in enumerate((zre, zim)):
                z[pl.ds((2 * kp + kpar) * NG, NG), :] = v[p * NG:(p + 1) * NG, kpar * LANES:(kpar + 1) * LANES]

    izv = iz[...]
    for ch in range(KPAD // ZCH):
        rows = pl.ds(ch * ZCH * NG, ZCH * NG)
        res = dot(cat([zre[rows, :], zim[rows, :]], 1).astype(jnp.bfloat16), izv)
        for kk in range(ZCH):
            k = ch * ZCH + kk
            for p in range(2):
                x2[pl.ds(p * KPAD + k, NG, stride=2 * KPAD), :] = res[kk * NG:(kk + 1) * NG, p * LANES:(p + 1) * LANES]

    xiv = xi[...]
    held = [None, None]
    first_part = None
    for yp in range(NG // 2):
        rhs = cat([x2[pl.ds((2 * yp + q) * 2 * KPAD, 2 * KPAD), :] for q in range(2)], 1).astype(jnp.bfloat16)
        res = dot(xiv, rhs)
        for q in range(2):
            for x0 in range(2):
                y = 2 * yp + q
                t, s = divmod(NG * (NG * x0 + y), LANES)
                v = res[x0 * KPAD:(x0 + 1) * KPAD, q * LANES:(q + 1) * LANES]
                r = pltpu.roll(v, s, 1) if s else v
                if held[x0] is None:
                    cur = r
                else:
                    cur = jnp.where(lane >= s, r, held[x0])
                if s + NG >= LANES:
                    if x0 == 1 and y == 0:
                        x2[pl.ds(0, KPAD), :] = cur
                    else:
                        flat[pl.ds(t, KPAD, stride=PAIR_ROWS), :] = cur
                    held[x0] = r
                else:
                    held[x0] = cur
    t, s = divmod(NG * NG, LANES)
    flat[pl.ds(t, KPAD, stride=PAIR_ROWS), :] = jnp.where(lane >= s, x2[pl.ds(0, KPAD), :], held[0])


def load_flat(src, dst, bands, grids):
    half = FLAT_ROWS // grids
    rows = src.shape[1]
    for g in range(grids):
        for c in range(bands):
            n = min(rows, half - c * rows)
            if n > 0:
                dst[pl.ds(g * half + c * rows, n), :] = src[c * grids + g, pl.ds(0, n), :].astype(jnp.float32)


def round_half(v):
    return v.astype(jnp.bfloat16).astype(jnp.float32)


def mix_kernel(order_row, order_col, localizer, x, out, spread):
    count = x.shape[0]
    groups, width = localizer.shape[0], localizer.shape[1]
    here = order_row[...] == lax.broadcasted_iota(jnp.int32, (count, count), 0)
    there = order_col[...] == lax.broadcasted_iota(jnp.int32, (count, count), 1)
    to_orbital = here.astype(jnp.float32).astype(jnp.bfloat16)
    from_orbital = there.astype(jnp.float32).astype(jnp.bfloat16)
    taken = [dot(localizer[g], from_orbital[g * width:(g + 1) * width]) for g in range(groups)]
    matrix = dot(to_orbital, cat(taken, 0).astype(jnp.bfloat16)).astype(jnp.bfloat16)
    rows = out.shape[1]
    for r in range(0, rows, 16):
        n = min(16, rows - r)
        y = dot(matrix, x[:, pl.ds(r * LANES, n * LANES)])
        for t in range(n):
            spread[pl.ds((r + t) * count, count), :] = y[:, t * LANES:(t + 1) * LANES]
    for o in range(count):
        out[o] = spread[pl.ds(o, rows, stride=count), :].astype(jnp.bfloat16)


def near_kernel(bands, grids, keep, own, near, xf, xi, fz, iz, yf, yi, kern,
                part, local, flat, other, zre, zim, s3, x2):
    position = lax.axis_index("band") * grids + lax.axis_index("grid")
    flag = keep[lax.rem(position + lax.rem(position + 1, 2), keep.shape[0])].astype(jnp.float32)
    load_flat(own, other.at[0], bands, grids)
    load_flat(near, other.at[1], bands, grids)
    flat[pl.ds(FLAT_ROWS, FLAT_ALLOC - FLAT_ROWS), :] = jnp.zeros((FLAT_ALLOC - FLAT_ROWS, LANES), jnp.float32)
    local[...] = other[0, pl.ds(0, FLAT_ROWS), :].astype(jnp.bfloat16)
    part[...] = jnp.zeros_like(part)

    def step(i, carry):
        flat[pl.ds(0, FLAT_ROWS), :] = round_half(other[0, pl.ds(0, FLAT_ROWS), :] * other[i, pl.ds(0, FLAT_ROWS), :])
        potential_in_flat(flat, zre, zim, s3, x2, (xf, xi, fz, iz, yf, yi, kern))
        scale = jnp.where(i == 0, 1.0, flag)
        part[...] += scale * flat[pl.ds(0, FLAT_ROWS), :] * other[i, pl.ds(0, FLAT_ROWS), :]
        return carry

    lax.fori_loop(0, 2, step, 0)


def far_kernel(bands, grids, keep, local, far, part, xf, xi, fz, iz, yf, yi, kern,
               out, flat, other, zre, zim, s3, x2):
    position = lax.axis_index("band") * grids + lax.axis_index("grid")
    flag = keep[lax.rem(position + lax.rem(position, 2), keep.shape[0])].astype(jnp.float32)
    load_flat(far, other, bands, grids)
    flat[pl.ds(FLAT_ROWS, FLAT_ALLOC - FLAT_ROWS), :] = jnp.zeros((FLAT_ALLOC - FLAT_ROWS, LANES), jnp.float32)
    flat[pl.ds(0, FLAT_ROWS), :] = round_half(local[...].astype(jnp.float32) * other[pl.ds(0, FLAT_ROWS), :])
    potential_in_flat(flat, zre, zim, s3, x2, (xf, xi, fz, iz, yf, yi, kern))
    out[...] = (part[...] + flag * flat[pl.ds(0, FLAT_ROWS), :] * other[pl.ds(0, FLAT_ROWS), :]).astype(jnp.bfloat16)


VM = pl.BlockSpec(memory_space=pltpu.VMEM)
SM = pl.BlockSpec(memory_space=pltpu.SMEM)


def work_areas():
    return [
        pltpu.VMEM(((KPAD + 1) * NG, LANES), jnp.float32),
        pltpu.VMEM(((KPAD + 1) * NG, LANES), jnp.float32),
        pltpu.VMEM((KPAD * NG, 2 * LANES), jnp.float32),
        pltpu.VMEM(((NG + 1) * 2 * KPAD, LANES), jnp.float32),
    ]


def cost(potentials):
    return pl.CostEstimate(flops=potentials * 2_000_000_000, bytes_accessed=potentials * 12_000_000, transcendentals=0)


def body(orbitals, group_order, localizer, bond_keep):
    bands, grids = lax.axis_size("band"), lax.axis_size("grid")
    count = bands * grids
    own_rows, half = orbitals.shape
    rows = -(-(half // LANES) // bands)
    rows = -(-rows // 8) * 8
    tables = tuple(jnp.asarray(t) for t in tables_np())
    keep = bond_keep.reshape(count)

    padded = jnp.pad(orbitals, ((0, 0), (0, bands * rows * LANES - half)))
    pieces = lax.all_to_all(
        padded.reshape(own_rows, bands, rows * LANES), "band", split_axis=1, concat_axis=1, tiled=True
    )
    pieces = jnp.transpose(pieces, (1, 0, 2)).reshape(count, rows * LANES)
    mixed = pl.pallas_call(
        mix_kernel,
        out_shape=jax.ShapeDtypeStruct((count, rows, LANES), jnp.bfloat16),
        in_specs=[VM] * 4,
        out_specs=VM,
        scratch_shapes=[pltpu.VMEM(((rows + 1) * count, LANES), jnp.float32)],
        name="mix",
    )(group_order.reshape(1, count), group_order.reshape(count, 1), localizer, pieces)
    own = lax.all_to_all(mixed, ("band", "grid"), split_axis=0, concat_axis=0, tiled=True)

    swap = []
    for i in range(1, count, 2):
        swap += [(i, (i + 1) % count), ((i + 1) % count, i)]
    far = lax.ppermute(own, ("band", "grid"), swap)
    near = lax.ppermute(own, "grid", [(0, 1), (1, 0)])

    flat_shape = jax.ShapeDtypeStruct((FLAT_ROWS, LANES), jnp.float32)
    half_shape = jax.ShapeDtypeStruct((FLAT_ROWS, LANES), jnp.bfloat16)
    part, local = pl.pallas_call(
        functools.partial(near_kernel, bands, grids),
        out_shape=(flat_shape, half_shape),
        in_specs=[SM] + [VM] * 9,
        out_specs=(VM, VM),
        scratch_shapes=[
            pltpu.VMEM((FLAT_ALLOC, LANES), jnp.float32),
            pltpu.VMEM((2, FLAT_ROWS + 4, LANES), jnp.float32),
        ] + work_areas(),
        cost_estimate=cost(2),
        name="near",
    )(keep, own, near, *tables)
    total = pl.pallas_call(
        functools.partial(far_kernel, bands, grids),
        out_shape=half_shape,
        in_specs=[SM] + [VM] * 10,
        out_specs=VM,
        scratch_shapes=[
            pltpu.VMEM((FLAT_ALLOC, LANES), jnp.float32),
            pltpu.VMEM((FLAT_ROWS + 4, LANES), jnp.float32),
        ] + work_areas(),
        cost_estimate=cost(1),
        name="far",
    )(keep, local, far, part, *tables)
    return local.reshape(1, -1), total.reshape(1, -1)


def solution(mesh):
    in_specs = (P(("mol", "band"), "grid"), P("mol"), P("mol", None, None), P("mol", None))
    out_specs = (P(("mol", "band", "grid"), None), P(("mol", "band", "grid"), None))
    return jax.shard_map(body, mesh=mesh, in_specs=in_specs, out_specs=out_specs, check_vma=False)
```

```python
import math, functools
import numpy as np
import jax, jax.numpy as jnp
from jax import lax
from jax.experimental import pallas as pl
from jax.experimental.pallas import tpu as pltpu
from jax.sharding import PartitionSpec as P

NG = 72
HC = NG // 2 + 1
LANES = 128
KPAD = 40
XPAIRS = NG // 2
PAIR_ROWS = 2 * NG * NG // LANES
FLAT_ROWS = NG * NG * NG // LANES
FLAT_ALLOC = PAIR_ROWS * (KPAD + 1) + 7
SCREEN = 0.0625

def tables_np():
    ang = lambda r, c: 2.0 * math.pi / NG * ((np.arange(r)[:, None] * np.arange(c)[None, :]) % NG)
    ax = ang(HC, NG)
    xt = np.stack([np.cos(ax), -np.sin(ax)])
    xf = np.zeros((2, KPAD, 2, KPAD))
    xf[:, :HC, :, :XPAIRS] = xt.reshape(2, HC, XPAIRS, 2).transpose(0, 1, 3, 2)
    xf = xf.reshape(2 * KPAD, 2 * KPAD)
    c, s = np.cos(ang(NG, NG)), np.sin(ang(NG, NG))
    def pad(b):
        out = np.zeros((2, LANES, 2, LANES))
        for i in range(2):
            for j in range(2):
                out[i, :NG, j, :NG] = b[i][j]
        return out.reshape(2 * LANES, 2 * LANES)
    fz = pad([[c, -s], [s, c]])
    iz = pad([[c, s], [-s, c]])
    yf = np.block([[c, s], [-s, c]])
    yi = np.block([[c, -s], [s, c]])
    sym = 4.0 * np.sin(math.pi / NG * np.arange(NG)) ** 2
    w = np.where((np.arange(HC) == 0) | (np.arange(HC) == NG // 2), 1.0, 2.0) / float(NG ** 3)
    kern = w[:, None, None] / (SCREEN + sym[:HC, None, None] + sym[None, :, None] + sym[None, None, :])
    kern[0, 0, 0] = 0.0
    kp = np.zeros((KPAD, NG, LANES))
    kp[:HC, :, :NG] = kern
    kp = kp.reshape(KPAD // 2, 2, NG, LANES).transpose(0, 2, 1, 3).reshape(KPAD // 2 * NG, 2 * LANES)
    b = lambda a: a.astype(np.float32).astype(jnp.bfloat16)
    return b(xf), b(xf.T), b(fz), b(iz), b(yf), b(yi), kp.astype(np.float32)

def dot(a, b):
    return jnp.dot(a, b, preferred_element_type=jnp.float32)

def cat(parts, axis):
    return jnp.concatenate(parts, axis=axis)

def potential_in_flat(flat, zre, zim, s3, x2, tabs, ZCH=10):
    xf, xi, fz, iz, yf, yi, kern = tabs
    lane = lax.broadcasted_iota(jnp.int32, (KPAD, LANES), 1)

    def piece(x0, y):
        t, s = divmod(NG * (NG * x0 + y), LANES)
        a = flat[pl.ds(t, KPAD, stride=PAIR_ROWS), :]
        if s + NG > LANES:
            b = flat[pl.ds(t + 1, KPAD, stride=PAIR_ROWS), :]
            a = jnp.where(lane >= s, a, b)
        if s:
            a = pltpu.roll(a, LANES - s, 1)
        return a

    xfv = xf[...]
    for yp in range(NG // 2):
        cols = [cat([piece(0, 2 * yp + q), piece(1, 2 * yp + q)], 0) for q in range(2)]
        res = dot(xfv, cat(cols, 1).astype(jnp.bfloat16))
        for q in range(2):
            for p, z in enumerate((zre, zim)):
                z[pl.ds(2 * yp + q, KPAD, stride=NG), :] = res[p * KPAD:(p + 1) * KPAD, q * LANES:(q + 1) * LANES]

    fzv = fz[...]
    for ch in range(KPAD // ZCH):
        rows = pl.ds(ch * ZCH * NG, ZCH * NG)
        res = dot(cat([zre[rows, :], zim[rows, :]], 1).astype(jnp.bfloat16), fzv)
        for kk in range(ZCH):
            kp, kpar = divmod(ch * ZCH + kk, 2)
            for p in range(2):
                s3[pl.ds(kp * 2 * NG + p * NG, NG), kpar * LANES:(kpar + 1) * LANES] = res[kk * NG:(kk + 1) * NG, p * LANES:(p + 1) * LANES]

    yfv, yiv = yf[...], yi[...]
    for kp in range(KPAD // 2):
        w = s3[pl.ds(kp * 2 * NG, 2 * NG), :].astype(jnp.bfloat16)
        t = dot(yfv, w)
        kk = kern[pl.ds(kp * NG, NG), :]
        t = cat([t[:NG] * kk, t[NG:] * kk], 0).astype(jnp.bfloat16)
        v = dot(yiv, t)
        for kpar in range(2):
            for p, z in enumerate((zre, zim)):
                z[pl.ds((2 * kp + kpar) * NG, NG), :] = v[p * NG:(p + 1) * NG, kpar * LANES:(kpar + 1) * LANES]

    izv = iz[...]
    for ch in range(KPAD // ZCH):
        rows = pl.ds(ch * ZCH * NG, ZCH * NG)
        res = dot(cat([zre[rows, :], zim[rows, :]], 1).astype(jnp.bfloat16), izv)
        for kk in range(ZCH):
            k = ch * ZCH + kk
            for p in range(2):
                x2[pl.ds(p * KPAD + k, NG, stride=2 * KPAD), :] = res[kk * NG:(kk + 1) * NG, p * LANES:(p + 1) * LANES]

    xiv = xi[...]
    held = [None, None]
    first_part = None
    for yp in range(NG // 2):
        rhs = cat([x2[pl.ds((2 * yp + q) * 2 * KPAD, 2 * KPAD), :] for q in range(2)], 1).astype(jnp.bfloat16)
        res = dot(xiv, rhs)
        for q in range(2):
            for x0 in range(2):
                y = 2 * yp + q
                t, s = divmod(NG * (NG * x0 + y), LANES)
                v = res[x0 * KPAD:(x0 + 1) * KPAD, q * LANES:(q + 1) * LANES]
                r = pltpu.roll(v, s, 1) if s else v
                if held[x0] is None:
                    cur = r
                else:
                    cur = jnp.where(lane >= s, r, held[x0])
                if s + NG >= LANES:
                    if x0 == 1 and y == 0:
                        x2[pl.ds(0, KPAD), :] = cur
                    else:
                        flat[pl.ds(t, KPAD, stride=PAIR_ROWS), :] = cur
                    held[x0] = r
                else:
                    held[x0] = cur
    t, s = divmod(NG * NG, LANES)
    flat[pl.ds(t, KPAD, stride=PAIR_ROWS), :] = jnp.where(lane >= s, x2[pl.ds(0, KPAD), :], held[0])


def load_flat(src, dst, bands, grids):
    half = FLAT_ROWS // grids
    rows = src.shape[1]
    for g in range(grids):
        for c in range(bands):
            n = min(rows, half - c * rows)
            if n > 0:
                dst[pl.ds(g * half + c * rows, n), :] = src[c * grids + g, pl.ds(0, n), :].astype(jnp.float32)


def round_half(v):
    return v.astype(jnp.bfloat16).astype(jnp.float32)


def fill_kernel(x, out, sem):
    half = x.shape[1]
    copy = pltpu.make_async_copy(x, out.at[:, pl.ds(0, half)], sem)
    copy.start()
    out[:, pl.ds(half, out.shape[1] - half)] = jnp.zeros((x.shape[0], out.shape[1] - half), jnp.bfloat16)
    copy.wait()


def mix_kernel(order_row, order_col, localizer, x, out, spread):
    count = x.shape[0]
    groups, width = localizer.shape[0], localizer.shape[1]
    here = order_row[...] == lax.broadcasted_iota(jnp.int32, (count, count), 0)
    there = order_col[...] == lax.broadcasted_iota(jnp.int32, (count, count), 1)
    to_orbital = here.astype(jnp.float32).astype(jnp.bfloat16)
    from_orbital = there.astype(jnp.float32).astype(jnp.bfloat16)
    taken = [dot(localizer[g], from_orbital[g * width:(g + 1) * width]) for g in range(groups)]
    matrix = dot(to_orbital, cat(taken, 0).astype(jnp.bfloat16))
    rows = out.shape[1]
    copies = max(1, min(8, 128 // count))
    if copies > 1:
        size = copies * count
        wide = cat([cat([matrix] * copies, 1)] * copies, 0)
        block = lambda d: lax.broadcasted_iota(jnp.int32, (size, size), d) // count
        matrix = jnp.where(block(0) == block(1), wide, 0.0)
    matrix = matrix.astype(jnp.bfloat16)
    span = rows // copies
    for r in range(0, span, 2):
        n = min(2, span - r)
        stacked = cat([x[:, pl.ds((j * span + r) * LANES, n * LANES)] for j in range(copies)], 0)
        y = dot(matrix, stacked)
        for j in range(copies):
            for t in range(n):
                spread[pl.ds((j * span + r + t) * count, count), :] = y[j * count:(j + 1) * count, t * LANES:(t + 1) * LANES]
    for o in range(count):
        out[o] = spread[pl.ds(o, rows, stride=count), :].astype(jnp.bfloat16)


def near_kernel(bands, grids, keep, own, near, xf, xi, fz, iz, yf, yi, kern,
                part, rounded, local, flat, other, zre, zim, s3, x2):
    position = lax.axis_index("band") * grids + lax.axis_index("grid")
    flag = keep[lax.rem(position + lax.rem(position + 1, 2), keep.shape[0])].astype(jnp.float32)
    load_flat(own, other.at[0], bands, grids)
    load_flat(near, other.at[1], bands, grids)
    flat[pl.ds(FLAT_ROWS, FLAT_ALLOC - FLAT_ROWS), :] = jnp.zeros((FLAT_ALLOC - FLAT_ROWS, LANES), jnp.float32)
    mine = other[0, pl.ds(0, FLAT_ROWS), :].astype(jnp.bfloat16)
    rounded[...] = mine
    local[...] = mine.reshape(local.shape)
    part[...] = jnp.zeros_like(part)

    def step(i, carry):
        flat[pl.ds(0, FLAT_ROWS), :] = round_half(other[0, pl.ds(0, FLAT_ROWS), :] * other[i, pl.ds(0, FLAT_ROWS), :])
        potential_in_flat(flat, zre, zim, s3, x2, (xf, xi, fz, iz, yf, yi, kern))
        scale = jnp.where(i == 0, 1.0, flag)
        part[...] += scale * flat[pl.ds(0, FLAT_ROWS), :] * other[i, pl.ds(0, FLAT_ROWS), :]
        return carry

    lax.fori_loop(0, 2, step, 0)


def far_kernel(bands, grids, keep, local, far, part, xf, xi, fz, iz, yf, yi, kern,
               out, flat, other, zre, zim, s3, x2):
    position = lax.axis_index("band") * grids + lax.axis_index("grid")
    flag = keep[lax.rem(position + lax.rem(position, 2), keep.shape[0])].astype(jnp.float32)
    load_flat(far, other, bands, grids)
    flat[pl.ds(FLAT_ROWS, FLAT_ALLOC - FLAT_ROWS), :] = jnp.zeros((FLAT_ALLOC - FLAT_ROWS, LANES), jnp.float32)
    flat[pl.ds(0, FLAT_ROWS), :] = round_half(local[...].astype(jnp.float32) * other[pl.ds(0, FLAT_ROWS), :])
    potential_in_flat(flat, zre, zim, s3, x2, (xf, xi, fz, iz, yf, yi, kern))
    total = part[...] + flag * flat[pl.ds(0, FLAT_ROWS), :] * other[pl.ds(0, FLAT_ROWS), :]
    out[...] = total.astype(jnp.bfloat16).reshape(out.shape)


VM = pl.BlockSpec(memory_space=pltpu.VMEM)
SM = pl.BlockSpec(memory_space=pltpu.SMEM)


def work_areas():
    return [
        pltpu.VMEM(((KPAD + 1) * NG, LANES), jnp.float32),
        pltpu.VMEM(((KPAD + 1) * NG, LANES), jnp.float32),
        pltpu.VMEM((KPAD * NG, 2 * LANES), jnp.float32),
        pltpu.VMEM(((NG + 1) * 2 * KPAD, LANES), jnp.float32),
    ]


def room(mib):
    return pltpu.CompilerParams(vmem_limit_bytes=mib * 1024 * 1024)


def cost(potentials):
    return pl.CostEstimate(flops=potentials * 2_000_000_000, bytes_accessed=potentials * 12_000_000, transcendentals=0)


def body(orbitals, group_order, localizer, bond_keep):
    bands, grids = lax.axis_size("band"), lax.axis_size("grid")
    count = bands * grids
    own_rows, half = orbitals.shape
    rows = -(-(half // LANES) // bands)
    rows = -(-rows // 8) * 8
    tables = tuple(jnp.asarray(t) for t in tables_np())
    keep = bond_keep.reshape(count)

    padded = pl.pallas_call(
        fill_kernel,
        out_shape=jax.ShapeDtypeStruct((own_rows, bands * rows * LANES), jnp.bfloat16),
        in_specs=[pl.BlockSpec(memory_space=pltpu.HBM)],
        out_specs=VM,
        scratch_shapes=[pltpu.SemaphoreType.DMA(())],
        compiler_params=room(8),
        name="fill",
    )(orbitals)
    pieces = lax.all_to_all(
        padded.reshape(own_rows, bands, rows * LANES), "band", split_axis=1, concat_axis=1, tiled=True
    )
    pieces = jnp.transpose(pieces, (1, 0, 2)).reshape(count, rows * LANES)
    mixed = pl.pallas_call(
        mix_kernel,
        out_shape=jax.ShapeDtypeStruct((count, rows, LANES), jnp.bfloat16),
        in_specs=[VM] * 4,
        out_specs=VM,
        scratch_shapes=[pltpu.VMEM(((rows + 1) * count, LANES), jnp.float32)],
        compiler_params=room(16),
        name="mix",
    )(group_order.reshape(1, count), group_order.reshape(count, 1), localizer, pieces)
    own = lax.all_to_all(mixed, ("band", "grid"), split_axis=0, concat_axis=0, tiled=True)

    swap = []
    for i in range(1, count, 2):
        swap += [(i, (i + 1) % count), ((i + 1) % count, i)]
    far = lax.ppermute(own, ("band", "grid"), swap)
    near = lax.ppermute(own, "grid", [(0, 1), (1, 0)])

    flat_shape = jax.ShapeDtypeStruct((FLAT_ROWS, LANES), jnp.float32)
    row_shape = jax.ShapeDtypeStruct((1, FLAT_ROWS * LANES), jnp.bfloat16)
    half_shape = jax.ShapeDtypeStruct((FLAT_ROWS, LANES), jnp.bfloat16)
    part, rounded, local = pl.pallas_call(
        functools.partial(near_kernel, bands, grids),
        out_shape=(flat_shape, half_shape, row_shape),
        in_specs=[SM] + [VM] * 9,
        out_specs=(VM, VM, VM),
        scratch_shapes=[
            pltpu.VMEM((FLAT_ALLOC, LANES), jnp.float32),
            pltpu.VMEM((2, FLAT_ROWS + 4, LANES), jnp.float32),
        ] + work_areas(),
        cost_estimate=cost(2),
        compiler_params=room(28),
        name="near",
    )(keep, own, near, *tables)
    total = pl.pallas_call(
        functools.partial(far_kernel, bands, grids),
        out_shape=row_shape,
        in_specs=[SM] + [VM] * 10,
        out_specs=VM,
        scratch_shapes=[
            pltpu.VMEM((FLAT_ALLOC, LANES), jnp.float32),
            pltpu.VMEM((FLAT_ROWS + 4, LANES), jnp.float32),
        ] + work_areas(),
        cost_estimate=cost(1),
        compiler_params=room(28),
        name="far",
    )(keep, rounded, far, part, *tables)
    return local, total


def solution(mesh):
    in_specs = (P(("mol", "band"), "grid"), P("mol"), P("mol", None, None), P("mol", None))
    out_specs = (P(("mol", "band", "grid"), None), P(("mol", "band", "grid"), None))
    return jax.shard_map(body, mesh=mesh, in_specs=in_specs, out_specs=out_specs, check_vma=False)
```

```python
import math, functools
import numpy as np
import jax, jax.numpy as jnp
from jax import lax
from jax.experimental import pallas as pl
from jax.experimental.pallas import tpu as pltpu
from jax.sharding import PartitionSpec as P

NG = 72
HC = NG // 2 + 1
LANES = 128
KPAD = 40
XPAIRS = NG // 2
PAIR_ROWS = 2 * NG * NG // LANES
FLAT_ROWS = NG * NG * NG // LANES
FLAT_ALLOC = PAIR_ROWS * (KPAD + 1) + 7
SCREEN = 0.0625

def tables_np():
    ang = lambda r, c: 2.0 * math.pi / NG * ((np.arange(r)[:, None] * np.arange(c)[None, :]) % NG)
    ax = ang(HC, NG)
    xt = np.stack([np.cos(ax), -np.sin(ax)])
    xf = np.zeros((2, KPAD, 2, KPAD))
    xf[:, :HC, :, :XPAIRS] = xt.reshape(2, HC, XPAIRS, 2).transpose(0, 1, 3, 2)
    xf = xf.reshape(2 * KPAD, 2 * KPAD)
    c, s = np.cos(ang(NG, NG)), np.sin(ang(NG, NG))
    def pad(b):
        out = np.zeros((2, LANES, 2, LANES))
        for i in range(2):
            for j in range(2):
                out[i, :NG, j, :NG] = b[i][j]
        return out.reshape(2 * LANES, 2 * LANES)
    fz = pad([[c, -s], [s, c]])
    iz = pad([[c, s], [-s, c]])
    yf = np.block([[c, s], [-s, c]])
    yi = np.block([[c, -s], [s, c]])
    sym = 4.0 * np.sin(math.pi / NG * np.arange(NG)) ** 2
    w = np.where((np.arange(HC) == 0) | (np.arange(HC) == NG // 2), 1.0, 2.0) / float(NG ** 3)
    kern = w[:, None, None] / (SCREEN + sym[:HC, None, None] + sym[None, :, None] + sym[None, None, :])
    kern[0, 0, 0] = 0.0
    kp = np.zeros((KPAD, NG, LANES))
    kp[:HC, :, :NG] = kern
    kp = kp.reshape(KPAD // 2, 2, NG, LANES).transpose(0, 2, 1, 3).reshape(KPAD // 2 * NG, 2 * LANES)
    b = lambda a: a.astype(np.float32).astype(jnp.bfloat16)
    return b(xf), b(xf.T), b(fz), b(iz), b(yf), b(yi), kp.astype(np.float32)

def dot(a, b):
    return jnp.dot(a, b, preferred_element_type=jnp.float32)

def cat(parts, axis):
    return jnp.concatenate(parts, axis=axis)

def potential_in_flat(flat, zre, zim, s3, x2, tabs, ZCH=10):
    xf, xi, fz, iz, yf, yi, kern = tabs
    lane = lax.broadcasted_iota(jnp.int32, (KPAD, LANES), 1)

    def piece(x0, y):
        t, s = divmod(NG * (NG * x0 + y), LANES)
        a = flat[pl.ds(t, KPAD, stride=PAIR_ROWS), :]
        if s + NG > LANES:
            b = flat[pl.ds(t + 1, KPAD, stride=PAIR_ROWS), :]
            a = jnp.where(lane >= s, a, b)
        if s:
            a = pltpu.roll(a, LANES - s, 1)
        return a

    xfv = xf[...]
    for yp in range(NG // 2):
        cols = [cat([piece(0, 2 * yp + q), piece(1, 2 * yp + q)], 0) for q in range(2)]
        res = dot(xfv, cat(cols, 1).astype(jnp.bfloat16))
        for q in range(2):
            for p, z in enumerate((zre, zim)):
                z[pl.ds(2 * yp + q, KPAD, stride=NG), :] = res[p * KPAD:(p + 1) * KPAD, q * LANES:(q + 1) * LANES]

    fzv = fz[...]
    for ch in range(KPAD // ZCH):
        rows = pl.ds(ch * ZCH * NG, ZCH * NG)
        res = dot(cat([zre[rows, :], zim[rows, :]], 1).astype(jnp.bfloat16), fzv)
        for kk in range(ZCH):
            kp, kpar = divmod(ch * ZCH + kk, 2)
            for p in range(2):
                s3[pl.ds(kp * 2 * NG + p * NG, NG), kpar * LANES:(kpar + 1) * LANES] = res[kk * NG:(kk + 1) * NG, p * LANES:(p + 1) * LANES]

    yfv, yiv = yf[...], yi[...]
    for kp in range(KPAD // 2):
        w = s3[pl.ds(kp * 2 * NG, 2 * NG), :].astype(jnp.bfloat16)
        t = dot(yfv, w)
        kk = kern[pl.ds(kp * NG, NG), :]
        t = cat([t[:NG] * kk, t[NG:] * kk], 0).astype(jnp.bfloat16)
        v = dot(yiv, t)
        for kpar in range(2):
            for p, z in enumerate((zre, zim)):
                z[pl.ds((2 * kp + kpar) * NG, NG), :] = v[p * NG:(p + 1) * NG, kpar * LANES:(kpar + 1) * LANES]

    izv = iz[...]
    for ch in range(KPAD // ZCH):
        rows = pl.ds(ch * ZCH * NG, ZCH * NG)
        res = dot(cat([zre[rows, :], zim[rows, :]], 1).astype(jnp.bfloat16), izv)
        for kk in range(ZCH):
            k = ch * ZCH + kk
            for p in range(2):
                x2[pl.ds(p * KPAD + k, NG, stride=2 * KPAD), :] = res[kk * NG:(kk + 1) * NG, p * LANES:(p + 1) * LANES]

    xiv = xi[...]
    held = [None, None]
    first_part = None
    for yp in range(NG // 2):
        rhs = cat([x2[pl.ds((2 * yp + q) * 2 * KPAD, 2 * KPAD), :] for q in range(2)], 1).astype(jnp.bfloat16)
        res = dot(xiv, rhs)
        for q in range(2):
            for x0 in range(2):
                y = 2 * yp + q
                t, s = divmod(NG * (NG * x0 + y), LANES)
                v = res[x0 * KPAD:(x0 + 1) * KPAD, q * LANES:(q + 1) * LANES]
                r = pltpu.roll(v, s, 1) if s else v
                if held[x0] is None:
                    cur = r
                else:
                    cur = jnp.where(lane >= s, r, held[x0])
                if s + NG >= LANES:
                    if x0 == 1 and y == 0:
                        x2[pl.ds(0, KPAD), :] = cur
                    else:
                        flat[pl.ds(t, KPAD, stride=PAIR_ROWS), :] = cur
                    held[x0] = r
                else:
                    held[x0] = cur
    t, s = divmod(NG * NG, LANES)
    flat[pl.ds(t, KPAD, stride=PAIR_ROWS), :] = jnp.where(lane >= s, x2[pl.ds(0, KPAD), :], held[0])


HALF_ROWS = FLAT_ROWS // 2
LISTED = 16


def band_index():
    return lax.axis_index("band")


def round_half(v):
    return v.astype(jnp.bfloat16).astype(jnp.float32)


def views(refs, bands):
    return list(refs) if bands <= LISTED else [refs[0].at[k] for k in range(bands)]


def cut_kernel(bands, x, *refs):
    outs, sems = views(refs[:-1], bands), refs[-1]
    size = outs[0].shape[1]
    full, rest = divmod(x.shape[1], size)

    def copy(k, place, length):
        return pltpu.make_async_copy(x.at[:, pl.ds(place, length)], outs[k].at[:, pl.ds(0, length)], sems.at[k])

    def each(act):
        for k in range(bands):
            other = jnp.bitwise_xor(band_index(), k)

            @pl.when(other < full)
            def _():
                act(copy(k, pl.multiple_of(other * size, LANES), size))

            if rest:
                @pl.when(other == full)
                def _():
                    act(copy(k, full * size, rest))

    for out in outs:
        if rest:
            out[:, pl.ds(rest, size - rest)] = jnp.zeros((x.shape[0], size - rest), jnp.bfloat16)
    each(lambda c: c.start())
    each(lambda c: c.wait())


def copies_of(count):
    return max(1, min(8, 128 // count))


def matrix_kernel(bands, order_row, order_col, localizer, out):
    count = order_row.shape[1]
    groups, width = localizer.shape[0], localizer.shape[1]
    twist = band_index() * (count // bands)
    index = lambda d: jnp.bitwise_xor(lax.broadcasted_iota(jnp.int32, (count, count), d), twist)
    to_orbital = (order_row[...] == index(0)).astype(jnp.float32).astype(jnp.bfloat16)
    from_orbital = (order_col[...] == index(1)).astype(jnp.float32).astype(jnp.bfloat16)
    taken = [dot(localizer[g], from_orbital[g * width:(g + 1) * width]) for g in range(groups)]
    matrix = dot(to_orbital, cat(taken, 0).astype(jnp.bfloat16))
    copies = copies_of(count)
    if copies > 1:
        size = copies * count
        wide = cat([cat([matrix] * copies, 1)] * copies, 0)
        block = lambda d: lax.broadcasted_iota(jnp.int32, (size, size), d) // count
        matrix = jnp.where(block(0) == block(1), wide, 0.0)
    out[...] = matrix.astype(jnp.bfloat16)


def mix_kernel(bands, weights, *refs):
    ends = bands if bands <= LISTED else 1
    sources, outs, (x, spread) = views(refs[:ends], bands), views(refs[ends:-2], bands), refs[-2:]
    count = x.shape[0]
    for k, source in enumerate(sources):
        x[pl.ds(k * source.shape[0], source.shape[0]), :] = source[...]
    matrix = weights[...]
    rows = outs[0].shape[1]
    copies = copies_of(count)
    span = rows // copies
    for r in range(0, span, 2):
        n = min(2, span - r)
        stacked = cat([x[:, pl.ds((j * span + r) * LANES, n * LANES)] for j in range(copies)], 0)
        y = dot(matrix, stacked)
        for j in range(copies):
            for t in range(n):
                spread[pl.ds((j * span + r + t) * count, count), :] = y[j * count:(j + 1) * count, t * LANES:(t + 1) * LANES]
    each = count // bands
    for k in range(bands):
        for o in range(each):
            outs[k][o] = spread[pl.ds(k * each + o, rows, stride=count), :].astype(jnp.bfloat16)


def join_kernel(bands, *refs):
    sources, (other, own) = views(refs[:-2], bands), refs[-2:]
    core = lax.axis_index("grid")
    for n, source in enumerate(sources):
        other[n] = source[1 - core]
        own[n] = source[core]


def place(source, dst, half, band):
    rows = source.shape[1]
    for k in range(source.shape[0]):
        at = pl.multiple_of(jnp.bitwise_xor(band, k) * rows, 8)
        dst[half, pl.ds(at, rows), :] = source[k].astype(jnp.float32)


def halves(fn):
    for h in range(2):
        fn(h, pl.ds(h * HALF_ROWS, HALF_ROWS), pl.ds(0, HALF_ROWS))


def clear_tail(flat):
    flat[pl.ds(FLAT_ROWS, FLAT_ALLOC - FLAT_ROWS), :] = jnp.zeros((FLAT_ALLOC - FLAT_ROWS, LANES), jnp.float32)


def near_kernel(keep, near_here, own_here, own_there, near_there, xf, xi, fz, iz, yf, yi, kern,
                part, rounded, local, flat, other, zre, zim, s3, x2):
    core, band = lax.axis_index("grid"), band_index()
    position = band * 2 + core
    flag = keep[lax.rem(position + 1 - core, keep.shape[0])].astype(jnp.float32)
    place(own_here, other.at[0], core, band)
    place(own_there, other.at[0], 1 - core, band)
    place(near_here, other.at[1], core, band)
    place(near_there, other.at[1], 1 - core, band)

    def lay(h, there, here):
        flat[there, :] = other[0, h, here, :]
    halves(lay)
    local[...] = flat[pl.ds(0, FLAT_ROWS), :].astype(jnp.bfloat16).reshape(local.shape)
    rounded[...] = other[0].astype(jnp.bfloat16)
    clear_tail(flat)
    part[...] = jnp.zeros_like(part)

    def step(i, carry):
        def density(h, there, here):
            flat[there, :] = round_half(other[0, h, here, :] * other[i, h, here, :])
        halves(density)
        potential_in_flat(flat, zre, zim, s3, x2, (xf, xi, fz, iz, yf, yi, kern))
        scale = jnp.where(i == 0, 1.0, flag)

        def add(h, there, here):
            part[h, here, :] += scale * flat[there, :] * other[i, h, here, :]
        halves(add)
        return carry

    lax.fori_loop(0, 2, step, 0)


def far_kernel(bands, keep, rounded, far_here, far_there, part, xf, xi, fz, iz, yf, yi, kern,
               out, flat, other, zre, zim, s3, x2):
    core, band = lax.axis_index("grid"), band_index()
    position = band * 2 + core
    flag = keep[lax.rem(position + core, keep.shape[0])].astype(jnp.float32)
    sender = lax.rem(band + bands - 1 + 2 * core, bands)
    place(far_here, other, core, sender)
    place(far_there, other, 1 - core, sender)
    clear_tail(flat)

    def density(h, there, here):
        flat[there, :] = round_half(rounded[h, here, :].astype(jnp.float32) * other[h, here, :])
    halves(density)
    potential_in_flat(flat, zre, zim, s3, x2, (xf, xi, fz, iz, yf, yi, kern))

    def add(h, there, here):
        flat[there, :] = part[h, here, :] + flag * flat[there, :] * other[h, here, :]
    halves(add)
    out[...] = flat[pl.ds(0, FLAT_ROWS), :].astype(jnp.bfloat16).reshape(out.shape)


VM = pl.BlockSpec(memory_space=pltpu.VMEM)
SM = pl.BlockSpec(memory_space=pltpu.SMEM)


def work_areas():
    return [
        pltpu.VMEM(((KPAD + 1) * NG, LANES), jnp.float32),
        pltpu.VMEM(((KPAD + 1) * NG, LANES), jnp.float32),
        pltpu.VMEM((KPAD * NG, 2 * LANES), jnp.float32),
        pltpu.VMEM(((NG + 1) * 2 * KPAD, LANES), jnp.float32),
    ]


def room(mib):
    return pltpu.CompilerParams(vmem_limit_bytes=mib * 1024 * 1024)


def cost(potentials):
    return pl.CostEstimate(flops=potentials * 2_000_000_000, bytes_accessed=potentials * 12_000_000, transcendentals=0)


def piece_shapes(bands, shape):
    if bands <= LISTED:
        return (jax.ShapeDtypeStruct(shape, jnp.bfloat16),) * bands
    return (jax.ShapeDtypeStruct((bands,) + shape, jnp.bfloat16),)


def exchange(pieces, bands):
    if bands <= LISTED:
        return (pieces[0],) + tuple(
            lax.ppermute(pieces[k], "band", [(i, i ^ k) for i in range(bands)]) for k in range(1, bands)
        )
    order = jnp.bitwise_xor(jnp.arange(bands, dtype=jnp.int32), band_index())
    moved = lax.all_to_all(pieces[0][order], "band", split_axis=0, concat_axis=0, tiled=True)
    return (moved[order],)


def body(orbitals, group_order, localizer, bond_keep):
    bands = lax.axis_size("band")
    count = bands * lax.axis_size("grid")
    own_rows = orbitals.shape[0]
    rows = -(-HALF_ROWS // bands)
    rows = -(-rows // 8) * 8
    tables = tuple(jnp.asarray(t) for t in tables_np())
    keep = bond_keep.reshape(count)

    cut = pl.pallas_call(
        functools.partial(cut_kernel, bands),
        out_shape=piece_shapes(bands, (own_rows, rows * LANES)),
        in_specs=[pl.BlockSpec(memory_space=pltpu.HBM)],
        out_specs=(VM,) * (bands if bands <= LISTED else 1),
        scratch_shapes=[pltpu.SemaphoreType.DMA((bands,))],
        compiler_params=room(8),
        name="cut",
    )(pltpu.with_memory_space_constraint(orbitals, pltpu.HBM))
    pieces = exchange(cut, bands)
    size = copies_of(count) * count
    weights = pl.pallas_call(
        functools.partial(matrix_kernel, bands),
        out_shape=jax.ShapeDtypeStruct((size, size), jnp.bfloat16),
        in_specs=[VM] * 3,
        out_specs=VM,
        compiler_params=room(8),
        name="matrix",
    )(group_order.reshape(1, count), group_order.reshape(count, 1), localizer)
    mixed = pl.pallas_call(
        functools.partial(mix_kernel, bands),
        out_shape=piece_shapes(bands, (own_rows, rows, LANES)),
        in_specs=[VM] * (1 + len(pieces)),
        out_specs=(VM,) * len(pieces),
        scratch_shapes=[pltpu.VMEM((count, rows * LANES), jnp.bfloat16), pltpu.VMEM(((rows + 1) * count, LANES), jnp.float32)],
        compiler_params=room(16),
        name="mix",
    )(weights, *pieces)
    arrived = exchange(mixed, bands)
    stack = jax.ShapeDtypeStruct((bands, rows, LANES), jnp.bfloat16)
    near_here, own_here = pl.pallas_call(
        functools.partial(join_kernel, bands),
        out_shape=(stack, stack),
        in_specs=[VM] * len(arrived),
        out_specs=(VM, VM),
        compiler_params=room(8),
        name="join",
    )(*arrived)

    first, second = [], []
    for b in range(bands):
        up, down = (b + 1) % bands, (b - 1) % bands
        first += [(2 * b, 2 * up), (2 * b + 1, 2 * down + 1)]
        second += [(2 * b + 1, 2 * up), (2 * b, 2 * down + 1)]
    far_here = lax.ppermute(near_here, ("band", "grid"), first)
    far_there = lax.ppermute(own_here, ("band", "grid"), second)
    own_there = lax.ppermute(near_here, "grid", [(0, 1), (1, 0)])
    near_there = lax.ppermute(own_here, "grid", [(0, 1), (1, 0)])

    row_shape = jax.ShapeDtypeStruct((1, FLAT_ROWS * LANES), jnp.bfloat16)
    part, rounded, local = pl.pallas_call(
        near_kernel,
        out_shape=(
            jax.ShapeDtypeStruct((2, bands * rows, LANES), jnp.float32),
            jax.ShapeDtypeStruct((2, bands * rows, LANES), jnp.bfloat16),
            row_shape,
        ),
        in_specs=[SM] + [VM] * 11,
        out_specs=(VM, VM, VM),
        scratch_shapes=[
            pltpu.VMEM((FLAT_ALLOC, LANES), jnp.float32),
            pltpu.VMEM((2, 2, bands * rows, LANES), jnp.float32),
        ] + work_areas(),
        cost_estimate=cost(2),
        compiler_params=room(28),
        name="near",
    )(keep, near_here, own_here, own_there, near_there, *tables)
    total = pl.pallas_call(
        functools.partial(far_kernel, bands),
        out_shape=row_shape,
        in_specs=[SM] + [VM] * 11,
        out_specs=VM,
        scratch_shapes=[
            pltpu.VMEM((FLAT_ALLOC, LANES), jnp.float32),
            pltpu.VMEM((2, bands * rows, LANES), jnp.float32),
        ] + work_areas(),
        cost_estimate=cost(1),
        compiler_params=room(28),
        name="far",
    )(keep, rounded, far_here, far_there, part, *tables)
    return local, total


def solution(mesh):
    in_specs = (P(("mol", "band"), "grid"), P("mol"), P("mol", None, None), P("mol", None))
    out_specs = (P(("mol", "band", "grid"), None), P(("mol", "band", "grid"), None))
    return jax.shard_map(body, mesh=mesh, in_specs=in_specs, out_specs=out_specs, check_vma=False)
```

```python
import math, functools
import numpy as np
import jax, jax.numpy as jnp
from jax import lax
from jax.experimental import pallas as pl
from jax.experimental.pallas import tpu as pltpu
from jax.sharding import PartitionSpec as P

NG = 72
HC = NG // 2 + 1
LANES = 128
KPAD = 40
XPAIRS = NG // 2
PAIR_ROWS = 2 * NG * NG // LANES
FLAT_ROWS = NG * NG * NG // LANES
FLAT_ALLOC = PAIR_ROWS * (KPAD + 1) + 7
SCREEN = 0.0625


def tables_np():
    ang = lambda r, c: 2.0 * math.pi / NG * ((np.arange(r)[:, None] * np.arange(c)[None, :]) % NG)
    ax = ang(HC, NG)
    xt = np.stack([np.cos(ax), -np.sin(ax)])
    xf = np.zeros((2, KPAD, 2, KPAD))
    xf[:, :HC, :, :XPAIRS] = xt.reshape(2, HC, XPAIRS, 2).transpose(0, 1, 3, 2)
    xf = xf.reshape(2 * KPAD, 2 * KPAD)
    c, s = np.cos(ang(NG, NG)), np.sin(ang(NG, NG))

    def pad(b):
        out = np.zeros((2, LANES, 2, LANES))
        for i in range(2):
            for j in range(2):
                out[i, :NG, j, :NG] = b[i][j]
        return out.reshape(2 * LANES, 2 * LANES)

    fz = pad([[c, -s], [s, c]])
    iz = pad([[c, s], [-s, c]])
    yf = np.block([[c, s], [-s, c]])
    yi = np.block([[c, -s], [s, c]])
    sym = 4.0 * np.sin(math.pi / NG * np.arange(NG)) ** 2
    w = np.where((np.arange(HC) == 0) | (np.arange(HC) == NG // 2), 1.0, 2.0) / float(NG ** 3)
    kern = w[:, None, None] / (SCREEN + sym[:HC, None, None] + sym[None, :, None] + sym[None, None, :])
    kern[0, 0, 0] = 0.0
    kp = np.zeros((KPAD, NG, LANES))
    kp[:HC, :, :NG] = kern
    kp = kp.reshape(KPAD // 2, 2, NG, LANES).transpose(0, 2, 1, 3).reshape(KPAD // 2 * NG, 2 * LANES)
    b = lambda a: a.astype(np.float32).astype(jnp.bfloat16)
    return b(xf), b(xf.T), b(fz), b(iz), b(yf), b(yi), kp.astype(np.float32)


def dot(a, b):
    return jnp.dot(a, b, preferred_element_type=jnp.float32)


def cat(parts, axis):
    return jnp.concatenate(parts, axis=axis)


def potential_in_flat(flat, zre, zim, s3, x2, tabs, ZCH=10):
    xf, xi, fz, iz, yf, yi, kern = tabs
    lane = lax.broadcasted_iota(jnp.int32, (KPAD, LANES), 1)

    def piece(x0, y):
        t, s = divmod(NG * (NG * x0 + y), LANES)
        a = flat[pl.ds(t, KPAD, stride=PAIR_ROWS), :]
        if s + NG > LANES:
            b = flat[pl.ds(t + 1, KPAD, stride=PAIR_ROWS), :]
            a = jnp.where(lane >= s, a, b)
        if s:
            a = pltpu.roll(a, LANES - s, 1)
        return a

    xfv = xf[...]
    for yp in range(NG // 2):
        cols = [cat([piece(0, 2 * yp + q), piece(1, 2 * yp + q)], 0) for q in range(2)]
        res = dot(xfv, cat(cols, 1).astype(jnp.bfloat16))
        for q in range(2):
            for p, z in enumerate((zre, zim)):
                z[pl.ds(2 * yp + q, KPAD, stride=NG), :] = res[p * KPAD:(p + 1) * KPAD, q * LANES:(q + 1) * LANES]

    fzv = fz[...]
    for ch in range(KPAD // ZCH):
        rows = pl.ds(ch * ZCH * NG, ZCH * NG)
        res = dot(cat([zre[rows, :], zim[rows, :]], 1).astype(jnp.bfloat16), fzv)
        for kk in range(ZCH):
            kp, kpar = divmod(ch * ZCH + kk, 2)
            for p in range(2):
                s3[pl.ds(kp * 2 * NG + p * NG, NG), kpar * LANES:(kpar + 1) * LANES] = res[kk * NG:(kk + 1) * NG, p * LANES:(p + 1) * LANES]

    yfv, yiv = yf[...], yi[...]
    for kp in range(KPAD // 2):
        w = s3[pl.ds(kp * 2 * NG, 2 * NG), :].astype(jnp.bfloat16)
        t = dot(yfv, w)
        kk = kern[pl.ds(kp * NG, NG), :]
        t = cat([t[:NG] * kk, t[NG:] * kk], 0).astype(jnp.bfloat16)
        v = dot(yiv, t)
        for kpar in range(2):
            for p, z in enumerate((zre, zim)):
                z[pl.ds((2 * kp + kpar) * NG, NG), :] = v[p * NG:(p + 1) * NG, kpar * LANES:(kpar + 1) * LANES]

    izv = iz[...]
    for ch in range(KPAD // ZCH):
        rows = pl.ds(ch * ZCH * NG, ZCH * NG)
        res = dot(cat([zre[rows, :], zim[rows, :]], 1).astype(jnp.bfloat16), izv)
        for kk in range(ZCH):
            k = ch * ZCH + kk
            for p in range(2):
                x2[pl.ds(p * KPAD + k, NG, stride=2 * KPAD), :] = res[kk * NG:(kk + 1) * NG, p * LANES:(p + 1) * LANES]

    xiv = xi[...]
    held = [None, None]
    for yp in range(NG // 2):
        rhs = cat([x2[pl.ds((2 * yp + q) * 2 * KPAD, 2 * KPAD), :] for q in range(2)], 1).astype(jnp.bfloat16)
        res = dot(xiv, rhs)
        for q in range(2):
            for x0 in range(2):
                y = 2 * yp + q
                t, s = divmod(NG * (NG * x0 + y), LANES)
                v = res[x0 * KPAD:(x0 + 1) * KPAD, q * LANES:(q + 1) * LANES]
                r = pltpu.roll(v, s, 1) if s else v
                if held[x0] is None:
                    cur = r
                else:
                    cur = jnp.where(lane >= s, r, held[x0])
                if s + NG >= LANES:
                    if x0 == 1 and y == 0:
                        x2[pl.ds(0, KPAD), :] = cur
                    else:
                        flat[pl.ds(t, KPAD, stride=PAIR_ROWS), :] = cur
                    held[x0] = r
                else:
                    held[x0] = cur
    t, s = divmod(NG * NG, LANES)
    flat[pl.ds(t, KPAD, stride=PAIR_ROWS), :] = jnp.where(lane >= s, x2[pl.ds(0, KPAD), :], held[0])


HALF_ROWS = FLAT_ROWS // 2
LISTED = 16


def band_index():
    return lax.axis_index("band")


def round_half(v):
    return v.astype(jnp.bfloat16).astype(jnp.float32)


def views(refs, bands):
    return list(refs) if bands <= LISTED else [refs[0].at[k] for k in range(bands)]


def cut_kernel(bands, x, *refs):
    outs, sems = views(refs[:-1], bands), refs[-1]
    size = outs[0].shape[1]
    full, rest = divmod(x.shape[1], size)

    def copy(k, place, length):
        return pltpu.make_async_copy(x.at[:, pl.ds(place, length)], outs[k].at[:, pl.ds(0, length)], sems.at[k])

    def each(act):
        for k in range(bands):
            other = jnp.bitwise_xor(band_index(), k)

            @pl.when(other < full)
            def _():
                act(copy(k, pl.multiple_of(other * size, LANES), size))

            if rest:
                @pl.when(other == full)
                def _():
                    act(copy(k, full * size, rest))

    for out in outs:
        if rest:
            out[:, pl.ds(rest, size - rest)] = jnp.zeros((x.shape[0], size - rest), jnp.bfloat16)
    each(lambda c: c.start())
    each(lambda c: c.wait())


def copies_of(count):
    return max(1, min(8, 128 // count))


def matrix_kernel(bands, order_row, order_col, localizer, out):
    count = order_row.shape[1]
    groups, width = localizer.shape[0], localizer.shape[1]
    twist = band_index() * (count // bands)
    index = lambda d: jnp.bitwise_xor(lax.broadcasted_iota(jnp.int32, (count, count), d), twist)
    to_orbital = (order_row[...] == index(0)).astype(jnp.float32).astype(jnp.bfloat16)
    from_orbital = (order_col[...] == index(1)).astype(jnp.float32).astype(jnp.bfloat16)
    taken = [dot(localizer[g], from_orbital[g * width:(g + 1) * width]) for g in range(groups)]
    matrix = dot(to_orbital, cat(taken, 0).astype(jnp.bfloat16))
    copies = copies_of(count)
    if copies > 1:
        size = copies * count
        wide = cat([cat([matrix] * copies, 1)] * copies, 0)
        block = lambda d: lax.broadcasted_iota(jnp.int32, (size, size), d) // count
        matrix = jnp.where(block(0) == block(1), wide, 0.0)
    out[...] = matrix.astype(jnp.bfloat16)


def mix_kernel(bands, weights, *refs):
    ends = bands if bands <= LISTED else 1
    sources, outs, (x, spread) = views(refs[:ends], bands), views(refs[ends:-2], bands), refs[-2:]
    count = x.shape[0]
    for k, source in enumerate(sources):
        x[pl.ds(k * source.shape[0], source.shape[0]), :] = source[...]
    matrix = weights[...]
    rows = outs[0].shape[1]
    copies = copies_of(count)
    span = rows // copies
    for r in range(0, span, 2):
        n = min(2, span - r)
        stacked = cat([x[:, pl.ds((j * span + r) * LANES, n * LANES)] for j in range(copies)], 0)
        y = dot(matrix, stacked)
        for j in range(copies):
            for t in range(n):
                spread[pl.ds((j * span + r + t) * count, count), :] = y[j * count:(j + 1) * count, t * LANES:(t + 1) * LANES]
    each = count // bands
    for k in range(bands):
        for o in range(each):
            outs[k][o] = spread[pl.ds(k * each + o, rows, stride=count), :].astype(jnp.bfloat16)


def join_kernel(bands, *refs):
    sources, (other, own) = views(refs[:-2], bands), refs[-2:]
    core = lax.axis_index("grid")
    for n, source in enumerate(sources):
        other[n] = source[1 - core]
        own[n] = source[core]


def place(source, dst, half, band):
    rows = source.shape[1]
    for k in range(source.shape[0]):
        at = pl.multiple_of(jnp.bitwise_xor(band, k) * rows, 8)
        dst[half, pl.ds(at, rows), :] = source[k].astype(jnp.float32)


def halves(fn):
    for h in range(2):
        fn(h, pl.ds(h * HALF_ROWS, HALF_ROWS), pl.ds(0, HALF_ROWS))


def clear_tail(flat):
    flat[pl.ds(FLAT_ROWS, FLAT_ALLOC - FLAT_ROWS), :] = jnp.zeros((FLAT_ALLOC - FLAT_ROWS, LANES), jnp.float32)


def near_kernel(keep, near_here, own_here, own_there, near_there, xf, xi, fz, iz, yf, yi, kern,
                part, rounded, local, flat, other, zre, zim, s3, x2):
    core, band = lax.axis_index("grid"), band_index()
    position = band * 2 + core
    flag = keep[lax.rem(position + 1 - core, keep.shape[0])].astype(jnp.float32)
    place(own_here, other.at[0], core, band)
    place(own_there, other.at[0], 1 - core, band)
    place(near_here, other.at[1], core, band)
    place(near_there, other.at[1], 1 - core, band)

    def lay(h, there, here):
        flat[there, :] = other[0, h, here, :]

    halves(lay)
    local[...] = flat[pl.ds(0, FLAT_ROWS), :].astype(jnp.bfloat16).reshape(local.shape)
    rounded[...] = other[0].astype(jnp.bfloat16)
    clear_tail(flat)
    part[...] = jnp.zeros_like(part)

    def step(i, carry):
        def density(h, there, here):
            flat[there, :] = round_half(other[0, h, here, :] * other[i, h, here, :])

        halves(density)
        potential_in_flat(flat, zre, zim, s3, x2, (xf, xi, fz, iz, yf, yi, kern))
        scale = jnp.where(i == 0, 1.0, flag)

        def add(h, there, here):
            part[h, here, :] += scale * flat[there, :] * other[i, h, here, :]

        halves(add)
        return carry

    lax.fori_loop(0, 2, step, 0)


def far_kernel(bands, keep, rounded, far_here, far_there, part, xf, xi, fz, iz, yf, yi, kern,
               out, flat, other, zre, zim, s3, x2):
    core, band = lax.axis_index("grid"), band_index()
    position = band * 2 + core
    flag = keep[lax.rem(position + core, keep.shape[0])].astype(jnp.float32)
    sender = lax.rem(band + bands - 1 + 2 * core, bands)
    place(far_here, other, core, sender)
    place(far_there, other, 1 - core, sender)
    clear_tail(flat)

    def density(h, there, here):
        flat[there, :] = round_half(rounded[h, here, :].astype(jnp.float32) * other[h, here, :])

    halves(density)
    potential_in_flat(flat, zre, zim, s3, x2, (xf, xi, fz, iz, yf, yi, kern))

    def add(h, there, here):
        flat[there, :] = part[h, here, :] + flag * flat[there, :] * other[h, here, :]

    halves(add)
    out[...] = flat[pl.ds(0, FLAT_ROWS), :].astype(jnp.bfloat16).reshape(out.shape)


VM = pl.BlockSpec(memory_space=pltpu.VMEM)
SM = pl.BlockSpec(memory_space=pltpu.SMEM)


def work_areas():
    return [
        pltpu.VMEM(((KPAD + 1) * NG, LANES), jnp.float32),
        pltpu.VMEM(((KPAD + 1) * NG, LANES), jnp.float32),
        pltpu.VMEM((KPAD * NG, 2 * LANES), jnp.float32),
        pltpu.VMEM(((NG + 1) * 2 * KPAD, LANES), jnp.float32),
    ]


def room(mib):
    return pltpu.CompilerParams(vmem_limit_bytes=mib * 1024 * 1024)


def cost(potentials):
    return pl.CostEstimate(flops=potentials * 2_000_000_000, bytes_accessed=potentials * 12_000_000, transcendentals=0)


def piece_shapes(bands, shape):
    if bands <= LISTED:
        return (jax.ShapeDtypeStruct(shape, jnp.bfloat16),) * bands
    return (jax.ShapeDtypeStruct((bands,) + shape, jnp.bfloat16),)


def exchange(pieces, bands):
    if bands <= LISTED:
        moved = {0: pieces[0]}
        for k in range(1, bands):
            moved[k] = lax.ppermute(pieces[k], "band", [(i, i ^ k) for i in range(bands)])
        return tuple(moved[k] for k in range(bands))
    order = jnp.bitwise_xor(jnp.arange(bands, dtype=jnp.int32), band_index())
    moved = lax.all_to_all(pieces[0][order], "band", split_axis=0, concat_axis=0, tiled=True)
    return (moved[order],)


def inner_body(orbitals, group_order, localizer, bond_keep):
    bands = lax.axis_size("band")
    count = bands * lax.axis_size("grid")
    own_rows = orbitals.shape[0]
    rows = -(-HALF_ROWS // bands)
    rows = -(-rows // 8) * 8
    tables = tuple(jnp.asarray(t) for t in tables_np())
    keep = bond_keep.reshape(count)

    cut = pl.pallas_call(
        functools.partial(cut_kernel, bands),
        out_shape=piece_shapes(bands, (own_rows, rows * LANES)),
        in_specs=[pl.BlockSpec(memory_space=pltpu.HBM)],
        out_specs=(VM,) * (bands if bands <= LISTED else 1),
        scratch_shapes=[pltpu.SemaphoreType.DMA((bands,))],
        compiler_params=room(8),
        name="cut",
    )(pltpu.with_memory_space_constraint(orbitals, pltpu.HBM))
    pieces = exchange(cut, bands)
    size = copies_of(count) * count
    weights = pl.pallas_call(
        functools.partial(matrix_kernel, bands),
        out_shape=jax.ShapeDtypeStruct((size, size), jnp.bfloat16),
        in_specs=[VM] * 3,
        out_specs=VM,
        compiler_params=room(8),
        name="matrix",
    )(group_order.reshape(1, count), group_order.reshape(count, 1), localizer)
    mixed = pl.pallas_call(
        functools.partial(mix_kernel, bands),
        out_shape=piece_shapes(bands, (own_rows, rows, LANES)),
        in_specs=[VM] * (1 + len(pieces)),
        out_specs=(VM,) * len(pieces),
        scratch_shapes=[pltpu.VMEM((count, rows * LANES), jnp.bfloat16), pltpu.VMEM(((rows + 1) * count, LANES), jnp.float32)],
        compiler_params=room(16),
        name="mix",
    )(weights, *pieces)
    arrived = exchange(mixed, bands)
    stack = jax.ShapeDtypeStruct((bands, rows, LANES), jnp.bfloat16)
    near_here, own_here = pl.pallas_call(
        functools.partial(join_kernel, bands),
        out_shape=(stack, stack),
        in_specs=[VM] * len(arrived),
        out_specs=(VM, VM),
        compiler_params=room(8),
        name="join",
    )(*arrived)

    first, second = [], []
    for b in range(bands):
        up, down = (b + 1) % bands, (b - 1) % bands
        first += [(2 * b, 2 * up), (2 * b + 1, 2 * down + 1)]
        second += [(2 * b + 1, 2 * up), (2 * b, 2 * down + 1)]
    far_here = lax.ppermute(near_here, ("band", "grid"), first)
    far_there = lax.ppermute(own_here, ("band", "grid"), second)
    own_there = lax.ppermute(near_here, "grid", [(0, 1), (1, 0)])
    near_there = lax.ppermute(own_here, "grid", [(0, 1), (1, 0)])

    row_shape = jax.ShapeDtypeStruct((1, FLAT_ROWS * LANES), jnp.bfloat16)
    part, rounded, local = pl.pallas_call(
        near_kernel,
        out_shape=(
            jax.ShapeDtypeStruct((2, bands * rows, LANES), jnp.float32),
            jax.ShapeDtypeStruct((2, bands * rows, LANES), jnp.bfloat16),
            row_shape,
        ),
        in_specs=[SM] + [VM] * 11,
        out_specs=(VM, VM, VM),
        scratch_shapes=[
            pltpu.VMEM((FLAT_ALLOC, LANES), jnp.float32),
            pltpu.VMEM((2, 2, bands * rows, LANES), jnp.float32),
        ] + work_areas(),
        cost_estimate=cost(2),
        compiler_params=room(28),
        name="near",
    )(keep, near_here, own_here, own_there, near_there, *tables)
    total = pl.pallas_call(
        functools.partial(far_kernel, bands),
        out_shape=row_shape,
        in_specs=[SM] + [VM] * 11,
        out_specs=VM,
        scratch_shapes=[
            pltpu.VMEM((FLAT_ALLOC, LANES), jnp.float32),
            pltpu.VMEM((2, bands * rows, LANES), jnp.float32),
        ] + work_areas(),
        cost_estimate=cost(1),
        compiler_params=room(28),
        name="far",
    )(keep, rounded, far_here, far_there, part, *tables)
    return local, total


def solution(mesh):
    in_specs = (P(("mol", "band"), "grid"), P("mol"), P("mol", None, None), P("mol", None))
    out_specs = (P(("mol", "band", "grid"), None), P(("mol", "band", "grid"), None))
    return jax.shard_map(inner_body, mesh=mesh, in_specs=in_specs, out_specs=out_specs, check_vma=False)
```
